32 devices in a mesh: band: 8 (over z, y), kpt: 4 (over x, core).
Axes of the slice: x: 2, y: 2, z: 4, core: 2. Of those that a mesh axis runs over, the one named last changes fastest.
Arguments:
- orbitals: float32 [8, 4, 2, 32, 768], P('band', 'kpt'), may hold values from -6 to 6
- screened_kernel: float32 [4, 32, 768], replicated, may hold values from 0.1 to 4
- kpoint_index: int32 [4], replicated, may hold values from 0 to 15, as said below
- q_index: int32 [16, 16], replicated, may hold values from 0 to 3
Outputs:
- exchange: float32 [8, 4, 2, 32, 768], P('band', 'kpt')
The draws below stay inside these ranges and needn't reach their ends.
Inputs may be any that keep to these rules, and one draw needn't show every extreme that they name: `kpoint_index`: the k-point numbers of the positions are all different.
All inputs are finite; a program needn't handle non-finite values.
Results may differ from the reference program's by a relative error of at most 0.0003.
Values sent between devices are 32-bit elements; how exact they have to be, the bound alone decides.
No kernel may reach another device: no remote copies, remote signals or barrier semaphores. Data moves between devices by JAX's collectives and lax.ppermute only.
A program may use at most 64 MiB of HBM per device.

```python
import math
import jax
import jax.numpy as jnp
from jax import lax

X = 32
Y = 32
Z = 24
NQ = 4
NBAND = 8
NKPT = 4
NKTAB = 16


def draw_kpoint_index(key, part):
    first_key = jax.random.fold_in(key, 11)
    second_key = jax.random.fold_in(key, 12)
    middle = 1 + jax.random.permutation(first_key, NKTAB - 2)[:NKPT - 2]
    values = jnp.concatenate([jnp.array([0, NKTAB - 1], dtype=jnp.int32), middle.astype(jnp.int32)])
    order = jax.random.permutation(second_key, NKPT)
    return values[order].astype(jnp.int32)


def plant(values, rng, low, largest):
    place = [jax.random.randint(jax.random.fold_in(rng, axis), (), 0, length) for axis, length in enumerate(values.shape)]
    widest = values.shape.index(max(values.shape))
    beside = place[:widest] + [(place[widest] + 1) % values.shape[widest]] + place[widest + 1:]
    return values.at[tuple(place)].set(low).at[tuple(beside)].set(largest)


def shard_levels(stream_key, shape, pieces, low, top_value):
    factor_of = 1.0
    for axis_at, shards_of in pieces:
        steps = jax.random.uniform(jax.random.fold_in(jax.random.fold_in(stream_key, 6), axis_at), (shards_of,), jnp.float32, low / len(pieces), top_value / len(pieces))
        factor_of = factor_of * jnp.repeat(jnp.exp(steps), shape[axis_at] // shards_of).reshape((-1,) + (1,) * (len(shape) - 1 - axis_at))
    return factor_of


def scatter_about(own_key, shape, deviation, limit, split=(), kind=jnp.bfloat16):
    loudness = shard_levels(own_key, shape, split, -0.22, 0.18) if split else 1.0
    drawn = jax.random.normal(own_key, shape, jnp.float32) * deviation * loudness
    return jnp.minimum(jnp.maximum(drawn, -limit), limit).astype(kind)


def setup_inputs(seed: int = 0) -> dict:
    key_list = jax.random.split(jax.random.key(seed), 5)
    orbitals = scatter_about(key_list[0], (NBAND, NKPT, 2, X, Y * Z), 1.0, 6.0, ((0, 8), (1, 4)), jnp.float32)
    screened_kernel = jnp.clip(jnp.exp(jax.random.uniform(key_list[1], (NQ, X, Y * Z), jnp.float32, math.log(0.1), math.log(4.0))), 0.1, 4.0)
    kpoint_index = draw_kpoint_index(jax.random.fold_in(key_list[4], 71), 0)
    q_index = plant(jax.random.randint(key_list[3], (NKTAB, NKTAB), 0, NQ), jax.random.fold_in(key_list[3], 1), 0, NQ - 1).astype(jnp.int32)
    return dict(orbitals=orbitals, screened_kernel=screened_kernel, kpoint_index=kpoint_index, q_index=q_index)


def pair_term(resident, visitor, weight, kernel_slab):
    res_real = resident[0].reshape(X, Y, Z)
    res_imag = resident[1].reshape(X, Y, Z)
    vis_real = visitor[0].reshape(X, Y, Z)
    vis_imag = visitor[1].reshape(X, Y, Z)
    density = (vis_real * res_real + vis_imag * res_imag) + 1j * (vis_real * res_imag - vis_imag * res_real)
    spectrum = jnp.fft.fftn(density) * kernel_slab.reshape(X, Y, Z)
    potential = jnp.fft.ifftn(spectrum)
    pot_real = jnp.real(potential)
    pot_imag = jnp.imag(potential)
    term_real = vis_real * pot_real - vis_imag * pot_imag
    term_imag = vis_real * pot_imag + vis_imag * pot_real
    return -weight * jnp.stack([term_real.reshape(X, Y * Z), term_imag.reshape(X, Y * Z)])


def reference(orbitals, screened_kernel, kpoint_index, q_index):
    weight = 1.0 / NKPT

    def one_band(band_row):
        rows = ((band_row + jnp.arange(-1, 2)) % NBAND).astype(jnp.int32)
        visitors = orbitals[rows]

        def one_resident(kpt_row):
            resident = orbitals[band_row, kpt_row]

            def one_visitor(visitor_number):
                offset = visitor_number // NKPT
                other = (visitor_number % NKPT).astype(jnp.int32)
                transfer = q_index[kpoint_index[kpt_row], kpoint_index[other]]
                return pair_term(resident, visitors[offset, other], weight, screened_kernel[transfer])

            terms = lax.map(one_visitor, jnp.arange(3 * NKPT, dtype=jnp.int32))
            return jnp.sum(terms, axis=0)

        return lax.map(one_resident, jnp.arange(NKPT, dtype=jnp.int32))

    return lax.map(one_band, jnp.arange(NBAND, dtype=jnp.int32))
```

```python
import functools
import math

import jax
import jax.numpy as jnp
import numpy as np
from jax import lax
from jax.experimental import pallas as pl
from jax.experimental.pallas import tpu as pltpu
from jax.sharding import PartitionSpec as P

Y = 32
Z = 24
LANES = 128
EIGHT = 8
THREE = Z // EIGHT
HIGH = Y // EIGHT
X = LANES // HIGH
ROWS = EIGHT * Z
POINTS = ROWS * LANES


def lane_table():
    high, x = np.arange(HIGH), np.arange(X)
    w_high = np.exp(-2j * np.pi * (np.outer(high, high) % HIGH) / HIGH)
    w_x = np.exp(-2j * np.pi * (np.outer(x, x) % X) / X)
    w = np.kron(w_high, w_x)
    table = np.block([[w.real, w.imag], [-w.imag, w.real]]).astype(np.float32)
    top = table.astype(jnp.bfloat16)
    rest = (table - top.astype(np.float32)).astype(jnp.bfloat16)
    return np.concatenate([top, top, rest], axis=0)


def twiddle_table():
    kz = np.arange(THREE)[:, None, None, None]
    low = np.arange(EIGHT)[None, :, None, None]
    s = np.arange(EIGHT)[None, None, :, None]
    k_high = (np.arange(LANES) // X)[None, None, None, :]
    turn = kz * s / Z + low * k_high / Y
    w = np.exp(-2j * np.pi * turn)
    return np.stack([w.real, w.imag]).astype(np.float32).reshape(2, ROWS, LANES)


def dft3(z):
    (ar, ai), (br, bi), (cr, ci) = z
    sr, si, dr, di = br + cr, bi + ci, br - cr, bi - ci
    mr, mi = ar - 0.5 * sr, ai - 0.5 * si
    h = math.sqrt(0.75)
    dr, di = h * dr, h * di
    return [(ar + sr, ai + si), (mr + di, mi - dr), (mr - di, mi + dr)]


def add(a, b):
    return a[0] + b[0], a[1] + b[1]


def sub(a, b):
    return a[0] - b[0], a[1] - b[1]


def add_turned(a, b):
    return a[0] + b[1], a[1] - b[0]


def sub_turned(a, b):
    return a[0] - b[1], a[1] + b[0]


def dft8(z):
    a0, a1, a2, a3 = add(z[0], z[4]), sub(z[0], z[4]), add(z[2], z[6]), sub(z[2], z[6])
    b0, b1, b2, b3 = add(z[1], z[5]), sub(z[1], z[5]), add(z[3], z[7]), sub(z[3], z[7])
    e0, e2, e1, e3 = add(a0, a2), sub(a0, a2), add_turned(a1, a3), sub_turned(a1, a3)
    o0, o2, o1, o3 = add(b0, b2), sub(b0, b2), add_turned(b1, b3), sub_turned(b1, b3)
    h = math.sqrt(0.5)
    p1 = (h * (o1[0] + o1[1]), h * (o1[1] - o1[0]))
    p3 = (h * (o3[1] - o3[0]), -h * (o3[0] + o3[1]))
    return [
        add(e0, o0), add(e1, p1), add_turned(e2, o2), add(e3, p3),
        sub(e0, o0), sub(e1, p1), sub_turned(e2, o2), sub(e3, p3),
    ]


def swapped(z):
    return [(b, a) for a, b in z]


def inverse8(z):
    return swapped(dft8(swapped(z)))


def inverse3(z):
    return swapped(dft3(swapped(z)))


def split(re, im):
    top_re, top_im = re.astype(jnp.bfloat16), im.astype(jnp.bfloat16)
    rest_re = (re - top_re.astype(jnp.float32)).astype(jnp.bfloat16)
    rest_im = (im - top_im.astype(jnp.float32)).astype(jnp.bfloat16)
    return top_re, top_im, rest_re, rest_im


def tile(index):
    return pl.ds(EIGHT * index, EIGHT)


def load(ref, rows):
    return ref[0, rows, :], ref[1, rows, :]


def store(ref, rows, value):
    ref[0, rows, :] = value[0]
    ref[1, rows, :] = value[1]


def put_split(lhs, rows, first, second):
    parts = split(first, second)
    for place, part in enumerate(parts):
        lhs[rows, place * LANES:(place + 1) * LANES] = part


def lane_dft(lhs, table):
    top = lhs[:, : 2 * LANES]
    rest = lhs[:, 2 * LANES:]
    return jnp.dot(
        jnp.concatenate([top, rest, top], axis=1), table[...], preferred_element_type=jnp.float32
    )


def pair(u, v, kernel, acc, fresh, tables, scratch):
    lane, twiddle = tables
    lhs, work = scratch
    step = 6 * EIGHT
    for start in range(0, ROWS, step):
        rows = pl.ds(start, step)
        ur, ui = load(u, rows)
        vr, vi = load(v, rows)
        put_split(lhs, rows, vr * ur + vi * ui, vr * ui - vi * ur)
    out = lane_dft(lhs, lane)
    for low in range(EIGHT):
        at = [EIGHT * (low * THREE + j) for j in range(THREE)]
        z = dft3([(out[a:a + EIGHT, :LANES], out[a:a + EIGHT, LANES:]) for a in at])
        for j in range(THREE):
            rows = tile(j * EIGHT + low)
            wr, wi = load(twiddle, rows)
            r, i = z[j]
            store(work, rows, (r * wr - i * wi, r * wi + i * wr))
    for j in range(THREE):
        z = dft8([load(work, tile(j * EIGHT + low)) for low in range(EIGHT)])
        for k in range(EIGHT):
            store(work, tile(j * EIGHT + k), z[k])
    for j in range(THREE):
        across = [pl.ds(j * EIGHT * EIGHT + s, EIGHT, stride=EIGHT) for s in range(EIGHT)]
        z = dft8([load(work, rows) for rows in across])
        scaled = []
        for k in range(EIGHT):
            weight = kernel[tile(j * EIGHT + k), :]
            scaled.append((z[k][0] * weight, z[k][1] * weight))
        z = inverse8(scaled)
        for s in range(EIGHT):
            store(work, across[s], z[s])
    for j in range(THREE):
        z = inverse8([load(work, tile(j * EIGHT + k)) for k in range(EIGHT)])
        for low in range(EIGHT):
            rows = tile(j * EIGHT + low)
            wr, wi = load(twiddle, rows)
            r, i = z[low]
            store(work, rows, (r * wr + i * wi, i * wr - r * wi))
    for low in range(0, EIGHT, 2):
        re, im = [], []
        for one in (low, low + 1):
            z = inverse3([load(work, tile(j * EIGHT + one)) for j in range(THREE)])
            re += [part[0] for part in z]
            im += [part[1] for part in z]
        put_split(
            lhs, pl.ds(low * Z, 2 * Z), jnp.concatenate(im, axis=0), jnp.concatenate(re, axis=0)
        )
    out = lane_dft(lhs, lane)
    for start in range(0, ROWS, step):
        rows = pl.ds(start, step)
        vr, vi = load(v, rows)
        pi, pr = out[start:start + step, :LANES], out[start:start + step, LANES:]
        value = (vr * pr - vi * pi, vr * pi + vi * pr)
        store(acc, rows, value if fresh else add(load(acc, rows), value))


def to_lanes(field):
    parts = [field[:, ROWS * h:ROWS * (h + 1)] for h in range(HIGH)]
    return jnp.concatenate(parts, axis=0).T


def from_lanes(field):
    turned = field.T
    return jnp.concatenate([turned[X * h:X * (h + 1), :] for h in range(HIGH)], axis=1)


def take_orbital(source, target):
    for part in range(2):
        target[part] = to_lanes(source[0, 0, part])


def take_kernel(slab, place, target):
    turned = slab.T.reshape(EIGHT, HIGH, Z, X)
    place[...] = jnp.concatenate([turned[:, h] for h in range(HIGH)], axis=-1).reshape(ROWS, LANES)
    for j in range(THREE):
        for k in range(EIGHT):
            target[tile(j * EIGHT + k), :] = place[pl.ds(j + THREE * k, EIGHT, stride=Z), :]


ORBITAL = jax.ShapeDtypeStruct((2, ROWS, LANES), jnp.float32)
VMEM = pl.BlockSpec(memory_space=pltpu.VMEM)
SMEM = pl.BlockSpec(memory_space=pltpu.SMEM)


def scratch_shapes(count):
    return [
        pltpu.VMEM((count, ROWS, 4 * LANES), jnp.bfloat16),
        pltpu.VMEM((count, 2, ROWS, LANES), jnp.float32),
    ]


def run(body, name, ins, outs, scratch, flops, specs=None):
    return pl.pallas_call(
        body,
        name=name,
        out_shape=outs,
        in_specs=specs or [VMEM] * len(ins),
        out_specs=[VMEM] * len(outs) if isinstance(outs, (list, tuple)) else VMEM,
        scratch_shapes=scratch,
        cost_estimate=pl.CostEstimate(flops=flops, bytes_accessed=1 << 20, transcendentals=0),
    )(*ins)


FLOPS_PAIR = 2 * ROWS * 768 * 256 * 2


def first_body(where, kpoint, q_index, own, partner, screened, lane, twiddle,
               own_t, partner_t, kernels, acc, lhs, work, place):
    here = where[0]
    other = where[1]
    take_orbital(own, own_t)
    take_orbital(partner, partner_t)
    for r, resident in enumerate((here, other)):
        for c, visitor in enumerate((here, where[2])):
            transfer = q_index[kpoint[resident], kpoint[visitor]]
            take_kernel(screened[transfer], place.at[2 * r + c], kernels.at[r, c])
    tables = (lane, twiddle)
    pair(own_t, own_t, kernels.at[0, 0], acc, True, tables, (lhs.at[0], work.at[0]))
    pair(own_t, partner_t, kernels.at[0, 1], acc, False, tables, (lhs.at[1], work.at[1]))


def second_body(across, near, own_t, partner_t, kernels, acc_in, lane, twiddle,
                across_t, near_t, acc, acc_x, lhs, work):
    take_orbital(across, across_t)
    take_orbital(near, near_t)
    tables = (lane, twiddle)
    acc[...] = acc_in[...]
    jobs = [
        (across_t, own_t, 1, 0, acc_x, True),
        (across_t, partner_t, 1, 1, acc_x, False),
        (across_t, near_t, 1, 0, acc_x, False),
        (own_t, near_t, 0, 0, acc, False),
    ]
    for n, (u, v, r, c, to, fresh) in enumerate(jobs):
        pair(u, v, kernels.at[r, c], to, fresh, tables, (lhs.at[n % 2], work.at[n % 2]))


def third_body(near, across_t, own_t, kernels, acc_in, acc_x_in, lane, twiddle,
               acc, acc_x, near_t, lhs, work):
    take_orbital(near, near_t)
    tables = (lane, twiddle)
    acc[...] = acc_in[...]
    acc_x[...] = acc_x_in[...]
    pair(across_t, near_t, kernels.at[1, 1], acc_x, False, tables, (lhs.at[0], work.at[0]))
    pair(own_t, near_t, kernels.at[0, 1], acc, False, tables, (lhs.at[1], work.at[1]))


def fourth_body(c, near, across_t, kernels, acc_x_in, lane, twiddle, near_t, acc_x, lhs, work):
    take_orbital(near, near_t)
    acc_x[...] = acc_x_in[...]
    pair(across_t, near_t, kernels.at[1, c], acc_x, False, (lane, twiddle), (lhs.at[0], work.at[0]))


def fifth_body(near_t, far_t, own_t, kernels, acc_in, lane, twiddle, acc, lhs, work):
    tables = (lane, twiddle)
    acc[...] = acc_in[...]
    pair(own_t, near_t, kernels.at[0, 0], acc, False, tables, (lhs.at[0], work.at[0]))
    pair(own_t, far_t, kernels.at[0, 1], acc, False, tables, (lhs.at[1], work.at[1]))


def last_body(scale, acc, back, out):
    for part in range(2):
        out[0, 0, part] = from_lanes(scale * (acc[part] + back[part]))


def local(mesh, orbitals, screened, kpoint, q_index):
    bands, kpts = mesh.shape["band"], mesh.shape["kpt"]
    scale = -1.0 / (kpts * POINTS)
    lane = jnp.asarray(lane_table())
    twiddle = jnp.asarray(twiddle_table())
    core = [(k, k ^ 1) for k in range(kpts)]
    across = [(k, (k + 2) % kpts) for k in range(kpts)]
    pairs_a = [(b, b ^ 1) for b in range(bands)]
    pairs_b = [(b, (b + 1 if b % 2 else b - 1) % bands) for b in range(bands)]
    here = lax.axis_index("kpt")
    where = jnp.stack([here, (here + 2) % kpts, here ^ 1]).astype(jnp.int32)

    partner = lax.ppermute(orbitals, "kpt", core)
    near_a = lax.ppermute(orbitals, "band", pairs_a)
    other = lax.ppermute(orbitals, "kpt", across)
    near_b = lax.ppermute(orbitals, "band", pairs_b)
    kernels = jax.ShapeDtypeStruct((2, 2, ROWS, LANES), jnp.float32)
    own_t, partner_t, kernels, acc = run(
        first_body, "first", (where, kpoint, q_index, orbitals, partner, screened, lane, twiddle),
        [ORBITAL, ORBITAL, kernels, ORBITAL],
        scratch_shapes(2) + [pltpu.VMEM((4, ROWS, LANES), jnp.float32)], 2 * FLOPS_PAIR,
        [SMEM] * 3 + [VMEM] * 5,
    )
    far_a = lax.ppermute(near_a, "kpt", core)
    other_t, near_t, acc, acc_x = run(
        second_body, "second", (other, near_a, own_t, partner_t, kernels, acc, lane, twiddle),
        [ORBITAL] * 4, scratch_shapes(2), 4 * FLOPS_PAIR,
    )
    acc, acc_x = run(
        third_body, "third", (far_a, other_t, own_t, kernels, acc, acc_x, lane, twiddle),
        [ORBITAL] * 2, [pltpu.VMEM((2, ROWS, LANES), jnp.float32)] + scratch_shapes(2), 2 * FLOPS_PAIR,
    )
    far_b = lax.ppermute(near_b, "kpt", core)
    near_t, acc_x = run(
        functools.partial(fourth_body, 0), "fourth", (near_b, other_t, kernels, acc_x, lane, twiddle),
        [ORBITAL] * 2, scratch_shapes(1), FLOPS_PAIR,
    )
    far_t, acc_x = run(
        functools.partial(fourth_body, 1), "fourth_far", (far_b, other_t, kernels, acc_x, lane, twiddle),
        [ORBITAL] * 2, scratch_shapes(1), FLOPS_PAIR,
    )
    back = lax.ppermute(acc_x, "kpt", across)
    acc = run(
        fifth_body, "fifth", (near_t, far_t, own_t, kernels, acc, lane, twiddle),
        ORBITAL, scratch_shapes(2), 2 * FLOPS_PAIR,
    )
    return run(
        functools.partial(last_body, scale), "last", (acc, back),
        jax.ShapeDtypeStruct(orbitals.shape, jnp.float32), [], 1 << 16,
    )


def solution(mesh):
    return jax.shard_map(
        functools.partial(local, mesh),
        mesh=mesh,
        in_specs=(P("band", "kpt", None, None, None), P(), P(), P()),
        out_specs=P("band", "kpt", None, None, None),
        check_vma=False,
    )
```
